512 devices in a mesh: ctx: 8 (over y_hi, x), head: 64 (over z, y_lo, core).
Axes of the slice: x: 4, y: 4 (y_hi: 2, y_lo: 2; y = y_hi * 2 + y_lo), z: 16, core: 2. Of those that a mesh axis runs over, the one named last changes fastest.
Arguments:
- queries: bfloat16 [4096, 8192], P('ctx', 'head'), may hold values from -6 to 6
- outputs: bfloat16 [4096, 8192], P('ctx', 'head'), may hold values from -6 to 6
- out_grad: bfloat16 [4096, 8192], P('ctx', 'head'), may hold values from -6 to 6
- keys_values: bfloat16 [2, 4096, 1024], P(None, 'ctx', 'head'), may hold values from -6 to 6
- row_lse: float32 [64, 4096], P('head', 'ctx'), may hold values from 4.5 to 6.5
- collide: int32 [64, 32, 8], P('head', 'ctx'), may hold values from 0 to 31, as said below
Outputs:
- query_grad: bfloat16 [4096, 8192], P('ctx', 'head')
- kv_grad: float32 [2, 4096, 1024], P(None, 'ctx', 'head')
The draws below stay inside these ranges and needn't reach their ends.
Inputs may be any that keep to these rules, and one draw needn't show every extreme that they name: Each row of collide names 8 different key blocks.
All inputs are finite; a program needn't handle non-finite values.
Results may differ from the reference program's by a relative error of at most 0.0042.
Values may be sent and summed in bfloat16 or wider, within the bound.
No kernel may reach another device: no remote copies, remote signals or barrier semaphores. Data moves between devices by JAX's collectives and lax.ppermute only.
A program may use at most 64 MiB of HBM per device.

```python
import jax
import jax.numpy as jnp
from jax import lax

H = 64
KVH = 8
DH = 128
BLOCK = 128
COLLIDE = 8
TOKENS = 4096
NQB = 32


def draw_collide(key, part):
    ranks = jax.random.randint(key, (H, NQB, NQB), 0, 1048576) * NQB + jnp.arange(NQB, dtype=jnp.int32)
    values, chosen = lax.top_k(ranks, COLLIDE)
    return chosen.astype(jnp.int32)


def shard_levels(own_key, extent, cuts, smallest, high):
    def one(dim, parts):
        heights = jax.random.uniform(jax.random.fold_in(jax.random.fold_in(own_key, 6), dim), (parts,), jnp.float32, smallest / len(cuts), high / len(cuts))
        return jnp.repeat(jnp.exp(heights), extent[dim] // parts).reshape((-1,) + (1,) * (len(extent) - dim - 1))

    loudness = one(*cuts[0])
    for cut in cuts[1:]:
        loudness = loudness * one(*cut)
    return loudness


def normal_values(stream_key, shape, scale, most, cuts=(), kind=jnp.bfloat16):
    factor_of = shard_levels(stream_key, shape, cuts, -0.22, 0.18) if cuts else 1.0
    result = jax.random.normal(stream_key, shape, jnp.float32) * scale * factor_of
    return jnp.minimum(jnp.maximum(result, -most), most).astype(kind)


def setup_inputs(seed: int = 0) -> dict:
    streams_of = jax.random.split(jax.random.key(seed), 7)
    queries = normal_values(streams_of[0], (TOKENS, H * DH), 1.0, 6.0, ((0, 8), (1, 64)))
    outputs = normal_values(streams_of[1], (TOKENS, H * DH), 1.0, 6.0, ((0, 8), (1, 64)))
    out_grad = normal_values(streams_of[2], (TOKENS, H * DH), 1.0, 6.0, ((0, 8), (1, 64)))
    keys_values = normal_values(streams_of[3], (2, TOKENS, KVH * DH), 1.0, 6.0, ((1, 8), (2, 64)))
    row_lse = jnp.clip(4.5 + 2.0 * jax.random.uniform(streams_of[4], (H, TOKENS), jnp.float32) ** shard_levels(streams_of[4], (H, TOKENS), ((0, 64), (1, 8)), -0.2, 0.2), 4.5, 6.5)
    collide = draw_collide(jax.random.fold_in(streams_of[6], 71), 0)
    return dict(queries=queries, outputs=outputs, out_grad=out_grad, keys_values=keys_values, row_lse=row_lse, collide=collide)


def tile_terms(query_blk, grad_blk, lse_blk, delta_blk, block_ids, key_blocks, value_blocks):
    score_scale = query_blk.shape[-1] ** -0.5
    key_tiles = key_blocks[block_ids]
    value_tiles = value_blocks[block_ids]
    query_f = query_blk.astype(jnp.float32)
    grad_f = grad_blk.astype(jnp.float32)
    scores = jnp.einsum('gid,grjd->grij', query_f, key_tiles.astype(jnp.float32)) * score_scale
    weights = jnp.exp(scores - lse_blk[:, None, :, None])
    weights_bf = weights.astype(jnp.bfloat16)
    value_grad = jnp.einsum('grij,gid->grjd', weights_bf.astype(jnp.float32), grad_f)
    weight_grad = jnp.einsum('gid,grjd->grij', grad_f, value_tiles.astype(jnp.float32))
    score_grad = (weights * (weight_grad - delta_blk[:, None, :, None]) * score_scale).astype(jnp.bfloat16)
    score_f = score_grad.astype(jnp.float32)
    query_grad = jnp.einsum('grij,grjd->gid', score_f, key_tiles.astype(jnp.float32)).astype(jnp.bfloat16)
    key_grad = jnp.einsum('grij,gid->grjd', score_f, query_f)
    return query_grad, key_grad, value_grad


def reference(queries, outputs, out_grad, keys_values, row_lse, collide):
    group_heads = H // KVH

    def head_step(totals, head_number):
        group_number = head_number // group_heads
        query_head = lax.dynamic_slice_in_dim(queries, head_number * DH, DH, 1).reshape(NQB // 2, 2, BLOCK, DH)
        grad_head = lax.dynamic_slice_in_dim(out_grad, head_number * DH, DH, 1)
        out_head = lax.dynamic_slice_in_dim(outputs, head_number * DH, DH, 1)
        delta_head = jnp.sum(grad_head.astype(jnp.float32) * out_head.astype(jnp.float32), axis=1).reshape(NQB // 2, 2, BLOCK)
        grad_head = grad_head.reshape(NQB // 2, 2, BLOCK, DH)
        lse_head = lax.dynamic_index_in_dim(row_lse, head_number, 0, keepdims=False).reshape(NQB // 2, 2, BLOCK)
        ids_head = lax.dynamic_index_in_dim(collide, head_number, 0, keepdims=False).reshape(NQB // 2, 2, COLLIDE)
        group_kv = lax.dynamic_slice_in_dim(keys_values, group_number * DH, DH, 2)
        key_blocks = group_kv[0].reshape(NQB, BLOCK, DH)
        value_blocks = group_kv[1].reshape(NQB, BLOCK, DH)
        group_totals = lax.dynamic_index_in_dim(totals, group_number, 0, keepdims=False)

        def pair_step(carry, items):
            query_blk, grad_blk, lse_blk, delta_blk, block_ids = items
            query_grad, key_grad, value_grad = tile_terms(query_blk, grad_blk, lse_blk, delta_blk, block_ids, key_blocks, value_blocks)
            flat_ids = block_ids.reshape(-1)
            carry = carry.at[0, flat_ids].add(key_grad.reshape(-1, BLOCK, DH))
            carry = carry.at[1, flat_ids].add(value_grad.reshape(-1, BLOCK, DH))
            return carry, query_grad

        group_totals, head_grads = lax.scan(pair_step, group_totals, (query_head, grad_head, lse_head, delta_head, ids_head))
        totals = lax.dynamic_update_index_in_dim(totals, group_totals, group_number, 0)
        return totals, head_grads.reshape(NQB, BLOCK, DH)

    start = jnp.zeros((KVH, 2, NQB, BLOCK, DH), jnp.float32)
    totals, all_grads = lax.scan(head_step, start, jnp.arange(H, dtype=jnp.int32))
    query_grad = all_grads.transpose(1, 2, 0, 3).reshape(TOKENS, H * DH)
    kv_grad = totals.transpose(1, 2, 3, 0, 4).reshape(2, TOKENS, KVH * DH)
    return query_grad, kv_grad
```

```python
import jax
import jax.numpy as jnp
from jax import lax
from jax.experimental import pallas as pl
from jax.experimental.pallas import tpu as pltpu
from jax.sharding import Mesh, PartitionSpec as P

KVH = 8
DH = 128
BLOCK = 128
F32 = jnp.float32
BF16 = jnp.bfloat16
I32 = jnp.int32
SCALE = DH ** -0.5
UNROLL = 4
CHIPS = ("yl", "zl", "x", "yh")
VMEM = pl.BlockSpec(memory_space=pltpu.VMEM)
SMEM = pl.BlockSpec(memory_space=pltpu.SMEM)
ROW_Q, ROW_G, ROW_O, ROW_S, ROW_KV, ROWS = 0, 512, 1024, 1536, 1552, 1616


def call(kernel, outs, in_specs, scratch=(), limit=24, name=None):
    return pl.pallas_call(
        kernel,
        out_shape=outs,
        in_specs=in_specs,
        out_specs=jax.tree.map(lambda _: VMEM, outs),
        scratch_shapes=list(scratch),
        compiler_params=pltpu.CompilerParams(vmem_limit_bytes=limit * 2**20),
        name=name,
    )


def pack_kernel(core_ref, q_ref, g_ref, o_ref, lse_ref, ids_ref, kv_ref, out_ref, small_ref):
    other = 1 - core_ref[0]
    out_ref[ROW_Q:ROW_G] = q_ref[...]
    out_ref[ROW_G:ROW_O] = g_ref[...]
    out_ref[ROW_O:ROW_S] = o_ref[...]
    lse = lse_ref[...]
    high = lse.astype(BF16).astype(F32)
    rest = lse - high
    middle = rest.astype(BF16).astype(F32)
    small_ref[...] = jnp.zeros((16, 128), F32)
    small_ref[0:4] = high
    small_ref[4:8] = middle
    small_ref[8:12] = rest - middle
    small_ref[12:16, 0:8] = ids_ref[...].astype(F32)
    out_ref[ROW_S:ROW_KV] = small_ref[...].astype(BF16)
    for which in range(2):
        for j in range(2):
            row = ROW_KV + (which * 2 + j) * 16
            out_ref[row : row + 16] = kv_ref[which, :, pl.ds(pl.multiple_of(other * 256 + j * 128, 128), 128)]


def spread_kernel(core_ref, kv_ref, pay_ref, out_ref):
    core = core_ref[0]
    for which in range(2):
        for j in range(2):
            own = kv_ref[which, :, pl.ds(pl.multiple_of(core * 256 + j * 128, 128), 128)]
            row = ROW_KV + (which * 2 + j) * 16
            got = pay_ref[row : row + 16]
            first = jnp.where(core == 0, own, got)
            second = jnp.where(core == 0, got, own)
            both = jnp.concatenate((first, second), 0)
            for chip in range(32):
                out_ref[chip, which, j] = both


def main_kernel(
    core_ref, ids_ref, q_ref, g_ref, o_ref, lse_ref, pay_ref, kv_ref,
    part_ref, dq_own_ref, dq_other_ref,
    q_all, g_all, q_t, g_t, lse_all, delta_all, acc, dq_acc, ids_v, ids_s, tiles, sem,
):
    core = core_ref[0]
    small = pay_ref[ROW_S:ROW_KV].astype(F32)
    ids_v[...] = small[8:16].astype(I32)
    copy = pltpu.make_async_copy(ids_v, ids_s, sem)
    copy.start()
    lse_other = small[0:4] + small[4:8] + small[8:12]
    lse_own = lse_ref[...]
    for b in range(8):
        rows = slice((b % 4) * 128, (b % 4) * 128 + 128)
        if b < 4:
            q, g, o = q_ref[rows], g_ref[rows], o_ref[rows]
            lse = lse_own[b : b + 1]
        else:
            at = (b - 4) * 128
            q = pay_ref[ROW_Q + at : ROW_Q + at + 128]
            g = pay_ref[ROW_G + at : ROW_G + at + 128]
            o = pay_ref[ROW_O + at : ROW_O + at + 128]
            lse = lse_other[b - 4 : b - 3]
        q_all[b] = q
        g_all[b] = g
        q_t[b] = q.T
        g_t[b] = g.T
        lse_all[b] = jnp.broadcast_to(lse, (128, 128)).T
        delta = jnp.sum(g.astype(F32) * o.astype(F32), axis=1, keepdims=True)
        delta_all[b] = jnp.broadcast_to(delta, (128, 128))
    acc[...] = jnp.zeros(acc.shape, F32)
    dq_acc[...] = jnp.zeros(dq_acc.shape, F32)
    copy.wait()
    count = jnp.int32(0)
    for b in range(8):
        for r in range(8):
            block = ids_ref[b, r] if b < 4 else ids_s[b, r]
            local = (block >> 2) * 2 + (block & 1)
            tiles[count] = b + local * 16 + b * 512 + local * 8192
            count = count + jnp.where(((block >> 1) & 1) == core, 1, 0)
    for u in range(UNROLL):
        tiles[count + u] = 8 * 512 + 16 * 8192

    def step(group, carry):
        items = []
        for u in range(UNROLL):
            word = tiles[group * UNROLL + u]
            b = word & 15
            local = (word >> 4) & 15
            yh, x, j = local >> 3, (local >> 1) & 3, local & 1
            k, v = (
                jnp.concatenate(
                    [kv_ref[yl, zl, x, yh, which, j] for zl in range(2) for yl in range(2)], 0
                )
                for which in range(2)
            )
            scores = jnp.dot(q_all[b], k, preferred_element_type=F32) * SCALE
            weights = jnp.exp(scores - lse_all[b])
            weight_grad = jnp.dot(g_all[b], v, preferred_element_type=F32)
            score_grad = (weights * (weight_grad - delta_all[b]) * SCALE).astype(BF16)
            weights_bf = weights.astype(BF16)
            dq = lax.dot_general(score_grad, k, (((1,), (1,)), ((), ())), preferred_element_type=F32)
            dk = jnp.dot(q_t[b], score_grad, preferred_element_type=F32)
            dv = jnp.dot(g_t[b], weights_bf, preferred_element_type=F32)
            items.append(((word >> 9) & 15, word >> 13, dq, dk, dv))
        for b, local, dq, dk, dv in items:
            dq_acc[b] += dq
            acc[local, 0] += dk
            acc[local, 1] += dv
        return carry

    lax.fori_loop(0, (count + UNROLL - 1) // UNROLL, step, 0)
    for b in range(4):
        dq_own_ref[b * 128 : b * 128 + 128] = dq_acc[b]
        dq_other_ref[b * 128 : b * 128 + 128] = dq_acc[b + 4]
    for yl in range(2):
        for zl in range(2):
            feature = (zl * 2 + yl) * 32
            for x in range(4):
                for yh in range(2):
                    for which in range(2):
                        for j in range(2):
                            local = (yh * 4 + x) * 2 + j
                            part_ref[yl, zl, x, yh, which, j] = acc[
                                local, which, feature : feature + 32
                            ].astype(BF16)


def sum_kernel(core_ref, got_ref, dq_other_ref, mine_ref, out_ref, total):
    core = core_ref[0]
    for t in range(4):
        value = got_ref[0, t].astype(F32)
        for chip in range(1, 32):
            value = value + got_ref[chip, t].astype(F32)
        total[t] = value
    out_ref[0:512] = dq_other_ref[...]
    for t in range(4):
        mine_ref[t] = total[t, pl.ds(pl.multiple_of(core * 16, 16), 16)]
        out_ref[512 + t * 16 : 528 + t * 16] = total[t, pl.ds(pl.multiple_of(16 - core * 16, 16), 16)]


def last_kernel(core_ref, mine_ref, got_ref, dq_ref, dq_out, kv_out):
    core = core_ref[0]
    dq_out[...] = (dq_ref[...] + got_ref[0:512]).astype(BF16)
    for which in range(2):
        for j in range(2):
            t = which * 2 + j
            own = mine_ref[t]
            got = got_ref[512 + t * 16 : 528 + t * 16]
            kv_out[which, :, j * 128 : j * 128 + 128] = jnp.where(core == 0, own, got)
            kv_out[which, :, 256 + j * 128 : 384 + j * 128] = jnp.where(core == 0, got, own)


def shards(queries, outputs, out_grad, keys_values, row_lse, collide):
    core = lax.axis_index("core").astype(I32).reshape(1)
    swap = [(0, 1), (1, 0)]
    kv = keys_values.transpose(0, 2, 1)
    lse = row_lse.reshape(4, BLOCK)
    ids = collide.reshape(4, 8)
    struct = jax.ShapeDtypeStruct
    packed = call(
        pack_kernel, struct((ROWS, DH), BF16), [SMEM] + [VMEM] * 6,
        [pltpu.VMEM((16, 128), F32)], name="pack",
    )(core, queries, out_grad, outputs, lse, ids, kv)
    pay = lax.ppermute(packed, "core", swap)
    spread = call(
        spread_kernel, struct((32, 2, 2, 32, 128), BF16), [SMEM, VMEM, VMEM], name="spread",
    )(core, kv, pay)
    gathered = lax.all_to_all(spread.reshape(32, 128, 128), CHIPS, 0, 0)
    part, dq_own, dq_other = call(
        main_kernel,
        (
            struct((2, 2, 4, 2, 2, 2, 32, 128), BF16),
            struct((512, DH), F32),
            struct((512, DH), F32),
        ),
        [SMEM, SMEM] + [VMEM] * 6,
        [pltpu.VMEM((8, 128, 128), BF16)] * 4
        + [pltpu.VMEM((8, 128, 128), F32)] * 2
        + [
            pltpu.VMEM((17, 2, 128, 128), F32),
            pltpu.VMEM((9, 128, 128), F32),
            pltpu.VMEM((8, 128), I32),
            pltpu.SMEM((8, 128), I32),
            pltpu.SMEM((72,), I32),
            pltpu.SemaphoreType.DMA,
        ],
        name="attend",
    )(core, ids, queries, out_grad, outputs, lse, pay, gathered.reshape(2, 2, 4, 2, 2, 2, 32, 128))
    got = lax.all_to_all(part.reshape(32, 128, 128), CHIPS, 0, 0)
    mine, back = call(
        sum_kernel, (struct((4, 16, 128), F32), struct((576, DH), F32)), [SMEM, VMEM, VMEM],
        [pltpu.VMEM((4, 32, 128), F32)], name="total",
    )(core, got.reshape(32, 4, 32, 128), dq_other)
    back = lax.ppermute(back, "core", swap)
    query_grad, kv_grad = call(
        last_kernel, (struct((512, DH), BF16), struct((2, 16, 512), F32)), [SMEM] + [VMEM] * 3,
        name="last",
    )(core, mine, back, dq_own)
    return query_grad, kv_grad.transpose(0, 2, 1)


def solution(mesh):
    fine = Mesh(
        mesh.devices.reshape(2, 4, KVH, 2, 2, 2), ("yh", "x", "group", "zl", "yl", "core")
    )
    ctx, head = ("yh", "x"), ("group", "zl", "yl", "core")
    placed = (
        P(ctx, head), P(ctx, head), P(ctx, head), P(None, ctx, head), P(head, ctx), P(head, ctx, None),
    )
    return jax.shard_map(
        shards, mesh=fine, in_specs=placed, out_specs=(P(ctx, head), P(None, ctx, head)),
        check_vma=False,
    )
```

```python
import jax
import jax.numpy as jnp
from jax import lax
from jax.experimental import pallas as pl
from jax.experimental.pallas import tpu as pltpu
from jax.sharding import Mesh, PartitionSpec as P

KVH = 8
DH = 128
BLOCK = 128
F32 = jnp.float32
BF16 = jnp.bfloat16
I32 = jnp.int32
SCALE = DH ** -0.5
PAIRS = 2
CHIPS = ("x", "yl", "zl", "yh")
HBM = pl.BlockSpec(memory_space=pltpu.MemorySpace.HBM)
VMEM = pl.BlockSpec(memory_space=pltpu.VMEM)
ROW_Q, ROW_G, ROW_S, ROWS = 0, 512, 1024, 1056


def call(kernel, outs, in_specs, scratch=(), limit=4, name=None):
    return pl.pallas_call(
        kernel,
        out_shape=outs,
        in_specs=in_specs,
        out_specs=jax.tree.map(lambda _: VMEM, outs),
        scratch_shapes=list(scratch),
        compiler_params=pltpu.CompilerParams(vmem_limit_bytes=limit * 2**20),
        name=name,
    )


def pieces(value):
    high = value.astype(BF16).astype(F32)
    rest = value - high
    middle = rest.astype(BF16).astype(F32)
    return high, middle, rest - middle


def pack_kernel(q_ref, g_ref, o_ref, lse_ref, ids_ref, out_ref, o_v, lse_v, ids_v, small, sems):
    copies = [
        pltpu.make_async_copy(source, target, sems.at[n])
        for n, (source, target) in enumerate((
            (lse_ref, lse_v),
            (ids_ref, ids_v),
            (q_ref, out_ref.at[ROW_Q:ROW_G]),
            (g_ref, out_ref.at[ROW_G:ROW_S]),
            (o_ref, o_v),
        ))
    ]
    for copy in copies:
        copy.start()
    small[...] = jnp.zeros((32, 128), F32)
    for copy in copies:
        copy.wait()
    lane = lax.broadcasted_iota(I32, (128, 128), 1)
    columns = jnp.zeros((128, 128), F32)
    for b in range(4):
        rows = slice(b * 128, b * 128 + 128)
        g = out_ref[ROW_G + b * 128 : ROW_G + b * 128 + 128]
        delta = jnp.sum(g.astype(F32) * o_v[rows].astype(F32), axis=1, keepdims=True)
        columns = jnp.where(lane == b, delta, columns)
    for n, piece in enumerate(pieces(lse_v[...]) + pieces(columns.T[0:4])):
        small[n * 4 : n * 4 + 4] = piece
    small[24:28, 0:8] = ids_v[...].astype(F32)
    out_ref[ROW_S:ROWS] = small[...].astype(BF16)


def stage_kernel(kv_ref, out_ref, sem):
    copy = pltpu.make_async_copy(kv_ref, out_ref, sem)
    copy.start()
    copy.wait()


def spread_kernel(own_ref, got_ref, out_ref):
    core = lax.axis_index("core")
    for which in range(2):
        for j in range(2):
            own_low, got_low = (ref[which, :, j * 128 : j * 128 + 128] for ref in (own_ref, got_ref))
            own_high, got_high = (ref[which, :, 256 + j * 128 : 384 + j * 128] for ref in (own_ref, got_ref))
            first = jnp.where(core == 0, own_low, got_high)
            second = jnp.where(core == 0, got_low, own_high)
            both = jnp.concatenate((first, second), 0)
            for chip in range(32):
                out_ref[chip, which, j] = both


NONE = 16
NO_PAIR = NONE + (8 << 14)


def ready_kernel(own_ref, got_ref, qg_ref, columns_ref, words_ref, table):
    core = lax.axis_index("core")
    table[...] = jnp.zeros((128, 128), F32)
    blocks = []
    for n, ref in enumerate((own_ref, got_ref)):
        small = ref[ROW_S:ROWS].astype(F32)
        table[n * 4 : n * 4 + 4] = small[0:4] + small[4:8] + small[8:12]
        table[8 + n * 4 : 12 + n * 4] = small[12:16] + small[16:20] + small[20:24]
        blocks.append(small[24:28])
        for b in range(4):
            qg_ref[n * 8 + b * 2] = ref[ROW_Q + b * 128 : ROW_Q + b * 128 + 128]
            qg_ref[n * 8 + b * 2 + 1] = ref[ROW_G + b * 128 : ROW_G + b * 128 + 128]
    columns_ref[...] = table[...].T
    block = jnp.concatenate(blocks, 0).astype(I32)
    row = lax.broadcasted_iota(I32, block.shape, 0)
    word = ((block >> 2) & 3) * 1024 + (block >> 4) * 128 + (block & 1) * 32
    word = word + (block >> 2) * 2 + (block & 1) + (row << 14) + (1 << 20)
    words_ref[...] = jnp.where(((block >> 1) & 1) == core, word, NONE)


def main_kernel(
    kv_ref, qg_ref, columns_ref, words_ref, part_ref, dq_own_ref, dq_other_ref,
    q_t, g_t, lse_all, delta_all, acc, dq_acc, held_w, held_s, words_s, slots, sem,
):
    copy = pltpu.make_async_copy(words_ref, words_s, sem)
    copy.start()
    for b in range(8):
        q_t[b] = qg_ref[b * 2].T
        g_t[b] = qg_ref[b * 2 + 1].T
    copy.wait()
    acc[...] = jnp.zeros(acc.shape, F32)
    dq_acc[...] = jnp.zeros(dq_acc.shape, F32)
    for b in range(8):
        lse_all[b] = jnp.broadcast_to(columns_ref[:, b : b + 1], (128, 128))
        delta_all[b] = jnp.broadcast_to(columns_ref[:, 8 + b : 9 + b], (128, 128))
    slot = jnp.int32(0)
    for b in range(8):
        for r in range(8):
            word = words_s[b, r]
            slots[slot] = word
            slot = slot + (word >> 20)
        slots[slot] = NONE
        slot = (slot + 1) & -2
    for p in range(4 * PAIRS):
        slots[slot + p] = NO_PAIR

    def tile(word, which):
        base = pl.multiple_of(word & 4064, 32)
        return jnp.concatenate(
            [
                kv_ref[pl.ds(base + yl * 512 + zl * 256 + which * 64, 32)]
                for zl in range(2)
                for yl in range(2)
            ],
            0,
        )

    def step(group, before):
        after, begun = [], []
        for u in range(PAIRS):
            at = (group * PAIRS + u) * 2
            one, two = slots[at], slots[at + 1]
            after += [one, two]
            b = (one >> 14) & 7
            k = jnp.concatenate((tile(one, 0), tile(two, 0)), 1)
            v = jnp.concatenate((tile(one, 1), tile(two, 1)), 1)
            scores = jnp.dot(qg_ref[b * 2], k, preferred_element_type=F32) * SCALE
            weight_grad = jnp.dot(qg_ref[b * 2 + 1], v, preferred_element_type=F32)
            lse, delta = lse_all[b], delta_all[b]
            for n in range(2):
                cols = slice(n * 128, n * 128 + 128)
                weights = jnp.exp(scores[:, cols] - lse)
                score_grad = (weights * (weight_grad[:, cols] - delta) * SCALE).astype(BF16)
                if n:
                    score_grad = jnp.where((two & 31) < NONE, score_grad, jnp.zeros_like(score_grad))
                begun.append((u, cols, weights.astype(BF16), score_grad))
        for u in range(PAIRS):
            one, two = before[u * 2 : u * 2 + 2]
            b = (one >> 14) & 15
            k = jnp.concatenate((tile(one, 0), tile(two, 0)), 1)
            score_grad = held_s[u]
            dq = lax.dot_general(score_grad, k, (((1,), (1,)), ((), ())), preferred_element_type=F32)
            dk = jnp.dot(q_t[b & 7], score_grad, preferred_element_type=F32)
            dv = jnp.dot(g_t[b & 7], held_w[u], preferred_element_type=F32)
            dq_acc[b] += dq
            first, second = one & 31, two & 31
            old = [acc[n, which] for n in (first, second) for which in range(2)]
            new = [dk[:, :128], dv[:, :128], dk[:, 128:], dv[:, 128:]]
            new = [x + y for x, y in zip(old, new)]
            acc[first, 0], acc[first, 1], acc[second, 0], acc[second, 1] = new
        for u, cols, weights, score_grad in begun:
            held_w[u, :, cols] = weights
            held_s[u, :, cols] = score_grad
        return tuple(after)

    steps = ((slot >> 1) + PAIRS - 1) // PAIRS + 1
    lax.fori_loop(0, steps, step, (jnp.int32(NO_PAIR),) * (2 * PAIRS))
    for b in range(4):
        dq_own_ref[b * 128 : b * 128 + 128] = dq_acc[b]
        dq_other_ref[b * 128 : b * 128 + 128] = dq_acc[b + 4]
    for x in range(4):
        for yl in range(2):
            for yh in range(2):
                for zl in range(2):
                    for which in range(2):
                        for j in range(2):
                            local = (yh * 4 + x) * 2 + j
                            at = x * 1024 + yl * 512 + zl * 256 + yh * 128 + which * 64 + j * 32
                            feature = (zl * 2 + yl) * 32
                            part_ref[at : at + 32] = acc[local, which, feature : feature + 32].astype(BF16)


def dq_kernel(own_ref, got_ref, out_ref):
    out_ref[...] = (own_ref[...] + got_ref[...]).astype(BF16)


def sum_kernel(got_ref, mine_ref, out_ref, total):
    core = lax.axis_index("core")
    for t in range(4):
        value = got_ref[0, t].astype(F32)
        for chip in range(1, 32):
            value = value + got_ref[chip, t].astype(F32)
        total[t] = value
    for t in range(4):
        mine_ref[t] = total[t, pl.ds(pl.multiple_of(core * 16, 16), 16)]
        out_ref[t] = total[t, pl.ds(pl.multiple_of(16 - core * 16, 16), 16)]


def last_kernel(mine_ref, got_ref, kv_out):
    core = lax.axis_index("core")
    for which in range(2):
        for j in range(2):
            own, got = mine_ref[which * 2 + j], got_ref[which * 2 + j]
            kv_out[which, :, j * 128 : j * 128 + 128] = jnp.where(core == 0, own, got)
            kv_out[which, :, 256 + j * 128 : 384 + j * 128] = jnp.where(core == 0, got, own)


def shards(queries, outputs, out_grad, keys_values, row_lse, collide):
    swap = [(0, 1), (1, 0)]
    struct = jax.ShapeDtypeStruct
    kv = keys_values.transpose(0, 2, 1)
    got_kv = lax.ppermute(kv, "core", swap)
    own_kv = call(stage_kernel, struct((2, 16, 512), BF16), [HBM], [pltpu.SemaphoreType.DMA], name="stage")(kv)
    spread = call(spread_kernel, struct((32, 2, 2, 32, 128), BF16), [VMEM] * 2, name="spread")(own_kv, got_kv)
    gathered = lax.all_to_all(spread.reshape(32, 128, 128), CHIPS, 0, 0)
    packed = call(
        pack_kernel, struct((ROWS, DH), BF16), [HBM] * 5,
        [
            pltpu.VMEM((512, DH), BF16),
            pltpu.VMEM((4, 128), F32),
            pltpu.VMEM((4, 8), I32),
            pltpu.VMEM((32, 128), F32),
            pltpu.SemaphoreType.DMA((5,)),
        ],
        name="pack",
    )(queries, out_grad, outputs, row_lse.reshape(4, BLOCK), collide.reshape(4, 8))
    pay = lax.ppermute(packed, "core", swap)
    ready = call(
        ready_kernel,
        (struct((16, 128, 128), BF16), struct((128, 128), F32), struct((8, 128), I32)),
        [VMEM] * 2, [pltpu.VMEM((128, 128), F32)], name="ready",
    )(packed, pay)
    part, dq_own, dq_other = call(
        main_kernel,
        (struct((4096, DH), BF16), struct((512, DH), F32), struct((512, DH), F32)),
        [VMEM] * 4,
        [pltpu.VMEM((8, 128, 128), BF16)] * 2
        + [pltpu.VMEM((8, 128, 128), F32)] * 2
        + [
            pltpu.VMEM((17, 2, 128, 128), F32),
            pltpu.VMEM((9, 128, 128), F32),
            pltpu.VMEM((PAIRS, 128, 256), BF16),
            pltpu.VMEM((PAIRS, 128, 256), BF16),
            pltpu.SMEM((8, 128), I32),
            pltpu.SMEM((64 + 16 + 4 * PAIRS,), I32),
            pltpu.SemaphoreType.DMA,
        ],
        name="attend",
        limit=16,
    )(gathered.reshape(4096, 128), *ready)
    got = lax.all_to_all(part.reshape(32, 128, 128), CHIPS, 0, 0)
    query_grad = call(dq_kernel, struct((512, DH), BF16), [VMEM] * 2, name="dq")(
        dq_own, lax.ppermute(dq_other, "core", swap)
    )
    mine, other = call(
        sum_kernel, (struct((4, 16, 128), F32),) * 2, [VMEM], [pltpu.VMEM((4, 32, 128), F32)], name="total",
    )(got.reshape(32, 4, 32, 128))
    kv_grad = call(last_kernel, struct((2, 16, 512), F32), [VMEM] * 2, name="last")(
        mine, lax.ppermute(other, "core", swap)
    )
    return query_grad, kv_grad.transpose(0, 2, 1)


def solution(mesh):
    fine = Mesh(
        mesh.devices.reshape(2, 4, KVH, 2, 2, 2), ("yh", "x", "group", "zl", "yl", "core")
    )
    ctx, head = ("yh", "x"), ("group", "zl", "yl", "core")
    placed = (
        P(ctx, head), P(ctx, head), P(ctx, head), P(None, ctx, head), P(head, ctx), P(head, ctx, None),
    )
    return jax.shard_map(
        shards, mesh=fine, in_specs=placed, out_specs=(P(ctx, head), P(None, ctx, head)),
        check_vma=False,
    )
```

```python
import jax
import jax.numpy as jnp
from jax import lax
from jax.experimental import pallas as pl
from jax.experimental.pallas import tpu as pltpu
from jax.sharding import Mesh, PartitionSpec as P

KVH = 8
DH = 128
BLOCK = 128
F32 = jnp.float32
BF16 = jnp.bfloat16
I32 = jnp.int32
SCALE = DH ** -0.5
PAIRS = 6
LOG2E = 1.4426950408889634
CHIPS = ("x", "yl", "zl", "yh")
HBM = pl.BlockSpec(memory_space=pltpu.MemorySpace.HBM)
VMEM = pl.BlockSpec(memory_space=pltpu.VMEM)
ROW_Q, ROW_G, ROW_S, ROWS = 0, 512, 1024, 1056


def call(kernel, outs, in_specs, scratch=(), limit=4, name=None):
    return pl.pallas_call(
        kernel,
        out_shape=outs,
        in_specs=in_specs,
        out_specs=jax.tree.map(lambda _: VMEM, outs),
        scratch_shapes=list(scratch),
        compiler_params=pltpu.CompilerParams(vmem_limit_bytes=limit * 2**20),
        name=name,
    )


def pieces(value):
    high = value.astype(BF16).astype(F32)
    rest = value - high
    middle = rest.astype(BF16).astype(F32)
    return high, middle, rest - middle


def pack_kernel(q_ref, g_ref, o_ref, lse_ref, ids_ref, out_ref, o_v, lse_v, ids_v, small, sems):
    copies = [
        pltpu.make_async_copy(source, target, sems.at[n])
        for n, (source, target) in enumerate((
            (lse_ref, lse_v),
            (ids_ref, ids_v),
            (q_ref, out_ref.at[ROW_Q:ROW_G]),
            (g_ref, out_ref.at[ROW_G:ROW_S]),
            (o_ref, o_v),
        ))
    ]
    for copy in copies:
        copy.start()
    small[...] = jnp.zeros((32, 128), F32)
    for copy in copies:
        copy.wait()
    lane = lax.broadcasted_iota(I32, (128, 128), 1)
    columns = jnp.zeros((128, 128), F32)
    for b in range(4):
        rows = slice(b * 128, b * 128 + 128)
        g = out_ref[ROW_G + b * 128 : ROW_G + b * 128 + 128]
        delta = jnp.sum(g.astype(F32) * o_v[rows].astype(F32), axis=1, keepdims=True)
        columns = jnp.where(lane == b, delta, columns)
    for n, piece in enumerate(pieces(lse_v[...]) + pieces(columns.T[0:4])):
        small[n * 4 : n * 4 + 4] = piece
    small[24:28, 0:8] = ids_v[...].astype(F32)
    out_ref[ROW_S:ROWS] = small[...].astype(BF16)


def stage_kernel(kv_ref, out_ref, sem):
    copy = pltpu.make_async_copy(kv_ref, out_ref, sem)
    copy.start()
    copy.wait()


def spread_kernel(own_ref, got_ref, out_ref):
    core = lax.axis_index("core")
    for which in range(2):
        for j in range(2):
            own_low, got_low = (ref[which, :, j * 128 : j * 128 + 128] for ref in (own_ref, got_ref))
            own_high, got_high = (ref[which, :, 256 + j * 128 : 384 + j * 128] for ref in (own_ref, got_ref))
            first = jnp.where(core == 0, own_low, got_high)
            second = jnp.where(core == 0, got_low, own_high)
            both = jnp.concatenate((first, second), 0)
            for chip in range(32):
                out_ref[chip, which, j] = both


NONE = 16
NO_PAIR = NONE + (8 << 14)


def ready_kernel(own_ref, got_ref, operands_ref, columns_ref, words_ref, table):
    core = lax.axis_index("core")
    table[...] = jnp.zeros((128, 128), F32)
    blocks = []
    for n, ref in enumerate((own_ref, got_ref)):
        small = ref[ROW_S:ROWS].astype(F32)
        table[n * 4 : n * 4 + 4] = (small[0:4] + small[4:8] + small[8:12]) * LOG2E
        table[8 + n * 4 : 12 + n * 4] = small[12:16] + small[16:20] + small[20:24]
        blocks.append(small[24:28])
        for b in range(4):
            for which, row in enumerate((ROW_Q, ROW_G)):
                value = ref[row + b * 128 : row + b * 128 + 128]
                operands_ref[n * 4 + b, which] = value
                operands_ref[n * 4 + b, 2 + which] = value.T
    columns_ref[...] = table[...].T
    block = jnp.concatenate(blocks, 0).astype(I32)
    row = lax.broadcasted_iota(I32, block.shape, 0)
    word = ((block >> 2) & 3) * 1024 + (block >> 4) * 128 + (block & 1) * 32
    word = word + (block >> 2) * 2 + (block & 1) + (row << 14) + (1 << 20)
    words_ref[...] = jnp.where(((block >> 1) & 1) == core, word, NONE)


def main_kernel(
    kv_ref, operands_ref, columns_ref, words_ref, part_ref, dq_own_ref, dq_other_ref,
    lse_all, delta_all, acc, dq_acc, words_s, slots, sem,
):
    copy = pltpu.make_async_copy(words_ref, words_s, sem)
    copy.start()
    for b in range(8):
        lse_all[b] = jnp.broadcast_to(columns_ref[:, b : b + 1], (128, 128))
        delta_all[b] = jnp.broadcast_to(columns_ref[:, 8 + b : 9 + b], (128, 128))
    copy.wait()
    acc[...] = jnp.zeros(acc.shape, F32)
    dq_acc[...] = jnp.zeros(dq_acc.shape, F32)
    slot = jnp.int32(0)
    for b in range(8):
        for r in range(8):
            word = words_s[b, r]
            slots[slot] = word
            slot = slot + (word >> 20)
        slots[slot] = NONE
        slot = (slot + 1) & -2
    for p in range(2 * PAIRS):
        slots[slot + p] = NO_PAIR

    def tiles(words, which):
        columns = []
        for word in words:
            base = pl.multiple_of(word & 4064, 32)
            rows = [
                kv_ref[pl.ds(base + yl * 512 + zl * 256 + which * 64, 32)]
                for zl in range(2)
                for yl in range(2)
            ]
            columns.append(jnp.concatenate(rows, 0))
        return jnp.concatenate(columns, 1)

    def step(group, carry):
        begun = []
        for u in range(PAIRS):
            at = (group * PAIRS + u) * 2
            words = slots[at], slots[at + 1]
            b = (words[0] >> 14) & 7
            k = tiles(words, 0)
            scores = jnp.dot(operands_ref[b, 0], k, preferred_element_type=F32)
            weight_grad = jnp.dot(operands_ref[b, 1], tiles(words, 1), preferred_element_type=F32)
            lse, delta = lse_all[b], delta_all[b]
            weights, score_grads = [], []
            for n in range(2):
                cols = slice(n * 128, n * 128 + 128)
                weight = jnp.exp2(scores[:, cols] * (SCALE * LOG2E) - lse)
                score_grad = (weight * (weight_grad[:, cols] - delta) * SCALE).astype(BF16)
                if n:
                    score_grad = jnp.where((words[1] & 31) < NONE, score_grad, jnp.zeros_like(score_grad))
                weights.append(weight.astype(BF16))
                score_grads.append(score_grad)
            begun.append((words, b, k, jnp.concatenate(weights, 1), jnp.concatenate(score_grads, 1)))
        for words, b, k, weights, score_grad in begun:
            dq = lax.dot_general(score_grad, k, (((1,), (1,)), ((), ())), preferred_element_type=F32)
            dk = jnp.dot(operands_ref[b, 2], score_grad, preferred_element_type=F32)
            dv = jnp.dot(operands_ref[b, 3], weights, preferred_element_type=F32)
            dq_acc[(words[0] >> 14) & 15] += dq
            first, second = words[0] & 31, words[1] & 31
            old = [acc[n, which] for n in (first, second) for which in range(2)]
            new = [dk[:, :128], dv[:, :128], dk[:, 128:], dv[:, 128:]]
            new = [x + y for x, y in zip(old, new)]
            acc[first, 0], acc[first, 1], acc[second, 0], acc[second, 1] = new
        return carry

    lax.fori_loop(0, ((slot >> 1) + PAIRS - 1) // PAIRS, step, 0)
    for b in range(4):
        dq_own_ref[b * 128 : b * 128 + 128] = dq_acc[b]
        dq_other_ref[b * 128 : b * 128 + 128] = dq_acc[b + 4]
    for x in range(4):
        for yl in range(2):
            for yh in range(2):
                for zl in range(2):
                    for which in range(2):
                        for j in range(2):
                            local = (yh * 4 + x) * 2 + j
                            at = x * 1024 + yl * 512 + zl * 256 + yh * 128 + which * 64 + j * 32
                            feature = (zl * 2 + yl) * 32
                            part_ref[at : at + 32] = acc[local, which, feature : feature + 32].astype(BF16)


def dq_kernel(own_ref, got_ref, out_ref):
    out_ref[...] = (own_ref[...] + got_ref[...]).astype(BF16)


def sum_kernel(got_ref, mine_ref, out_ref, total):
    core = lax.axis_index("core")
    for t in range(4):
        value = got_ref[0, t].astype(F32)
        for chip in range(1, 32):
            value = value + got_ref[chip, t].astype(F32)
        total[t] = value
    for t in range(4):
        mine_ref[t] = total[t, pl.ds(pl.multiple_of(core * 16, 16), 16)]
        out_ref[t] = total[t, pl.ds(pl.multiple_of(16 - core * 16, 16), 16)]


def last_kernel(mine_ref, got_ref, kv_out):
    core = lax.axis_index("core")
    for which in range(2):
        for j in range(2):
            own, got = mine_ref[which * 2 + j], got_ref[which * 2 + j]
            kv_out[which, :, j * 128 : j * 128 + 128] = jnp.where(core == 0, own, got)
            kv_out[which, :, 256 + j * 128 : 384 + j * 128] = jnp.where(core == 0, got, own)


def shards(queries, outputs, out_grad, keys_values, row_lse, collide):
    swap = [(0, 1), (1, 0)]
    struct = jax.ShapeDtypeStruct
    kv = keys_values.transpose(0, 2, 1)
    got_kv = lax.ppermute(kv, "core", swap)
    own_kv = call(stage_kernel, struct((2, 16, 512), BF16), [HBM], [pltpu.SemaphoreType.DMA], name="stage")(kv)
    spread = call(spread_kernel, struct((32, 2, 2, 32, 128), BF16), [VMEM] * 2, name="spread")(own_kv, got_kv)
    gathered = lax.all_to_all(spread.reshape(32, 128, 128), CHIPS, 0, 0)
    packed = call(
        pack_kernel, struct((ROWS, DH), BF16), [HBM] * 5,
        [
            pltpu.VMEM((512, DH), BF16),
            pltpu.VMEM((4, 128), F32),
            pltpu.VMEM((4, 8), I32),
            pltpu.VMEM((32, 128), F32),
            pltpu.SemaphoreType.DMA((5,)),
        ],
        name="pack",
    )(queries, out_grad, outputs, row_lse.reshape(4, BLOCK), collide.reshape(4, 8))
    pay = lax.ppermute(packed, "core", swap)
    ready = call(
        ready_kernel,
        (struct((8, 4, 128, 128), BF16), struct((128, 128), F32), struct((8, 128), I32)),
        [VMEM] * 2, [pltpu.VMEM((128, 128), F32)], name="ready",
    )(packed, pay)
    part, dq_own, dq_other = call(
        main_kernel,
        (struct((4096, DH), BF16), struct((512, DH), F32), struct((512, DH), F32)),
        [VMEM] * 4,
        [
            pltpu.VMEM((8, 128, 128), F32),
            pltpu.VMEM((8, 128, 128), F32),
            pltpu.VMEM((17, 2, 128, 128), F32),
            pltpu.VMEM((9, 128, 128), F32),
            pltpu.SMEM((8, 128), I32),
            pltpu.SMEM((64 + 16 + 2 * PAIRS,), I32),
            pltpu.SemaphoreType.DMA,
        ],
        name="attend",
        limit=16,
    )(gathered.reshape(4096, 128), *ready)
    got = lax.all_to_all(part.reshape(32, 128, 128), CHIPS, 0, 0)
    query_grad = call(dq_kernel, struct((512, DH), BF16), [VMEM] * 2, name="dq")(
        dq_own, lax.ppermute(dq_other, "core", swap)
    )
    mine, other = call(
        sum_kernel, (struct((4, 16, 128), F32),) * 2, [VMEM], [pltpu.VMEM((4, 32, 128), F32)], name="total",
    )(got.reshape(32, 4, 32, 128))
    kv_grad = call(last_kernel, struct((2, 16, 512), F32), [VMEM] * 2, name="last")(
        mine, lax.ppermute(other, "core", swap)
    )
    return query_grad, kv_grad.transpose(0, 2, 1)


def solution(mesh):
    fine = Mesh(
        mesh.devices.reshape(2, 4, KVH, 2, 2, 2), ("yh", "x", "group", "zl", "yl", "core")
    )
    ctx, head = ("yh", "x"), ("group", "zl", "yl", "core")
    placed = (
        P(ctx, head), P(ctx, head), P(ctx, head), P(None, ctx, head), P(head, ctx), P(head, ctx, None),
    )
    return jax.shard_map(
        shards, mesh=fine, in_specs=placed, out_specs=(P(ctx, head), P(None, ctx, head)),
        check_vma=False,
    )
```

```python
import jax
import jax.numpy as jnp
from jax import lax
from jax.experimental import pallas as pl
from jax.experimental.pallas import tpu as pltpu
from jax.sharding import Mesh, PartitionSpec as P

KVH = 8
DH = 128
BLOCK = 128
F32 = jnp.float32
BF16 = jnp.bfloat16
I32 = jnp.int32
SCALE = DH ** -0.5
PAIRS = 6
LOG2E = 1.4426950408889634
DEVICES = ("x", "yl", "zl", "yh", "core")
HBM = pl.BlockSpec(memory_space=pltpu.MemorySpace.HBM)
VMEM = pl.BlockSpec(memory_space=pltpu.VMEM)
ROW_Q, ROW_G, ROW_S, ROWS = 0, 512, 1024, 1056


def call(kernel, outs, in_specs, scratch=(), limit=4, name=None, outs_at=None):
    return pl.pallas_call(
        kernel,
        out_shape=outs,
        in_specs=in_specs,
        out_specs=outs_at or jax.tree.map(lambda _: VMEM, outs),
        scratch_shapes=list(scratch),
        compiler_params=pltpu.CompilerParams(vmem_limit_bytes=limit * 2**20),
        name=name,
    )


def pieces(value):
    high = value.astype(BF16).astype(F32)
    rest = value - high
    middle = rest.astype(BF16).astype(F32)
    return high, middle, rest - middle


def pack_kernel(q_ref, g_ref, o_ref, lse_ref, ids_ref, out_ref, o_v, lse_v, ids_v, small, sems):
    copies = [
        pltpu.make_async_copy(source, target, sems.at[n])
        for n, (source, target) in enumerate((
            (lse_ref, lse_v),
            (ids_ref, ids_v),
            (q_ref, out_ref.at[ROW_Q:ROW_G]),
            (g_ref, out_ref.at[ROW_G:ROW_S]),
            (o_ref, o_v),
        ))
    ]
    for copy in copies:
        copy.start()
    small[...] = jnp.zeros((32, 128), F32)
    for copy in copies:
        copy.wait()
    lane = lax.broadcasted_iota(I32, (128, 128), 1)
    columns = jnp.zeros((128, 128), F32)
    for b in range(4):
        rows = slice(b * 128, b * 128 + 128)
        g = out_ref[ROW_G + b * 128 : ROW_G + b * 128 + 128]
        delta = jnp.sum(g.astype(F32) * o_v[rows].astype(F32), axis=1, keepdims=True)
        columns = jnp.where(lane == b, delta, columns)
    for n, piece in enumerate(pieces(lse_v[...]) + pieces(columns.T[0:4])):
        small[n * 4 : n * 4 + 4] = piece
    small[24:28, 0:8] = ids_v[...].astype(F32)
    out_ref[ROW_S:ROWS] = small[...].astype(BF16)


def spread_kernel(kv_ref, out_ref, chunk, sems):
    for half in range(2):
        for which in range(2):
            for j in range(2):
                at = half * 64 + which * 32 + j * 16
                column = half * 256 + j * 128
                value = kv_ref[which, :, column : column + 128]
                for chip in range(8):
                    chunk[chip, at : at + 16] = value
    copies = [
        pltpu.make_async_copy(chunk, out_ref.at[n * 8 : n * 8 + 8], sems.at[n]) for n in range(4)
    ]
    for copy in copies:
        copy.start()
    for copy in copies:
        copy.wait()


SPAN = 880
NONE = 16
NO_PAIR = NONE + (8 << 14)


def ready_kernel(own_ref, got_ref, operands_ref, columns_ref, words_ref, table):
    core = lax.axis_index("core")
    table[...] = jnp.zeros((128, 128), F32)
    blocks = []
    for n, ref in enumerate((own_ref, got_ref)):
        small = ref[ROW_S:ROWS].astype(F32)
        lse = (small[0:4] + small[4:8] + small[8:12]) * LOG2E
        delta = small[12:16] + small[16:20] + small[20:24]
        blocks.append(small[24:28])
        for b in range(4):
            for which, row in enumerate((ROW_Q, ROW_G)):
                value = ref[row + b * 128 : row + b * 128 + 128]
                operands_ref[n * 4 + b, which] = value
                operands_ref[n * 4 + b, 2 + which] = value.T
            table[0:1] = lse[b : b + 1]
            table[1:2] = delta[b : b + 1]
            columns_ref[n * 4 + b] = table[...].T
    block = jnp.concatenate(blocks, 0).astype(I32)
    row = lax.broadcasted_iota(I32, block.shape, 0)
    word = (((block >> 2) & 3) * 1024 + (block >> 4) * 128 + (block & 1) * 16) * 2
    word = word + (block >> 2) * 2 + (block & 1) + (row << 14) + (1 << 20)
    words_ref[...] = jnp.where(((block >> 1) & 1) == core, word, NONE)


def main_kernel(
    kv_ref, operands_ref, columns_ref, words_ref, part_ref, dq_own_ref, dq_other_ref,
    acc, dq_acc, part, words_s, slots, sem, part_sems,
):
    copy = pltpu.make_async_copy(words_ref, words_s, sem)
    copy.start()
    dq_acc[...] = jnp.zeros(dq_acc.shape, F32)
    acc[0:8] = jnp.zeros((8,) + acc.shape[1:], F32)
    copy.wait()
    acc[8:17] = jnp.zeros((9,) + acc.shape[1:], F32)
    slot = jnp.int32(0)
    for b in range(8):
        for r in range(8):
            word = words_s[b, r]
            slots[slot] = word
            slot = slot + (word >> 20)
        slots[slot] = NONE
        slot = (slot + 1) & -2
    for p in range(2 * PAIRS):
        slots[slot + p] = NO_PAIR

    def tiles(words, which):
        columns = []
        for word in words:
            block = kv_ref.at[pl.ds(pl.multiple_of((word & 8160) >> 1, 16), SPAN)]
            rows = [
                block[yl * 512 + zl * 256 + core * 64 + which * 32 : yl * 512 + zl * 256 + core * 64 + which * 32 + 16]
                for zl in range(2)
                for yl in range(2)
                for core in range(2)
            ]
            columns.append(jnp.concatenate(rows, 0))
        return jnp.concatenate(columns, 1)

    def step(group, carry):
        begun = []
        for u in range(PAIRS):
            at = (group * PAIRS + u) * 2
            words = slots[at], slots[at + 1]
            b = (words[0] >> 14) & 7
            k = tiles(words, 0)
            scores = jnp.dot(operands_ref[b, 0], k, preferred_element_type=F32)
            weight_grad = jnp.dot(operands_ref[b, 1], tiles(words, 1), preferred_element_type=F32)
            lse, delta = (
                jnp.broadcast_to(columns_ref[b, :, n : n + 1], (128, 128)) for n in range(2)
            )
            weights, score_grads = [], []
            for n in range(2):
                cols = slice(n * 128, n * 128 + 128)
                weight = jnp.exp2(scores[:, cols] * (SCALE * LOG2E) - lse)
                score_grad = (weight * (weight_grad[:, cols] - delta) * SCALE).astype(BF16)
                if n:
                    score_grad = jnp.where((words[1] & 31) < NONE, score_grad, jnp.zeros_like(score_grad))
                weights.append(weight.astype(BF16))
                score_grads.append(score_grad)
            begun.append((words, b, k, jnp.concatenate(weights, 1), jnp.concatenate(score_grads, 1)))
        for words, b, k, weights, score_grad in begun:
            dq = lax.dot_general(score_grad, k, (((1,), (1,)), ((), ())), preferred_element_type=F32)
            dk = jnp.dot(operands_ref[b, 2], score_grad, preferred_element_type=F32)
            dv = jnp.dot(operands_ref[b, 3], weights, preferred_element_type=F32)
            dq_acc[(words[0] >> 14) & 15] += dq
            first, second = words[0] & 31, words[1] & 31
            old = [acc[n, which] for n in (first, second) for which in range(2)]
            new = [dk[:, :128], dv[:, :128], dk[:, 128:], dv[:, 128:]]
            new = [x + y for x, y in zip(old, new)]
            acc[first, 0], acc[first, 1], acc[second, 0], acc[second, 1] = new
        return carry

    lax.fori_loop(0, ((slot >> 1) + PAIRS - 1) // PAIRS, step, 0)
    copies = []
    for x in range(4):
        for yl in range(2):
            for zl in range(2):
                for yh in range(2):
                    for core in range(2):
                        for which in range(2):
                            for j in range(2):
                                at = x * 1024 + yl * 512 + zl * 256 + yh * 128 + core * 64 + which * 32 + j * 16
                                feature = (zl * 2 + yl) * 32 + core * 16
                                tile = acc[(yh * 4 + x) * 2 + j, which, feature : feature + 16]
                                part[at : at + 16] = tile.astype(BF16)
        rows = slice(x * 1024, x * 1024 + 1024)
        copies.append(pltpu.make_async_copy(part.at[rows], part_ref.at[rows], part_sems.at[x]))
        copies[-1].start()
    for b in range(4):
        dq_own_ref[b * 128 : b * 128 + 128] = dq_acc[b]
        dq_other_ref[b * 128 : b * 128 + 128] = dq_acc[b + 4]
    for copy in copies:
        copy.wait()


def dq_kernel(own_ref, got_ref, out_ref):
    out_ref[...] = (own_ref[...] + got_ref[...]).astype(BF16)


def sum_kernel(got_ref, out_ref):
    for core in range(2):
        for which in range(2):
            for j in range(2):
                at = core * 64 + which * 32 + j * 16
                value = got_ref[0, at : at + 16].astype(F32)
                for chip in range(1, 32):
                    value = value + got_ref[chip, at : at + 16].astype(F32)
                column = core * 256 + j * 128
                out_ref[which, :, column : column + 128] = value


def shards(queries, outputs, out_grad, keys_values, row_lse, collide):
    swap = [(0, 1), (1, 0)]
    struct = jax.ShapeDtypeStruct
    spread = call(
        spread_kernel, struct((32, 128, 128), BF16), [VMEM],
        [pltpu.VMEM((8, 128, 128), BF16), pltpu.SemaphoreType.DMA((4,))],
        name="spread", outs_at=HBM,
    )(keys_values.transpose(0, 2, 1))

    def exchange(value):
        return lax.all_to_all(value.reshape(64, 64, 128), DEVICES, 0, 0)

    gathered = exchange(spread)
    packed = call(
        pack_kernel, struct((ROWS, DH), BF16), [HBM] * 5,
        [
            pltpu.VMEM((512, DH), BF16),
            pltpu.VMEM((4, 128), F32),
            pltpu.VMEM((4, 8), I32),
            pltpu.VMEM((32, 128), F32),
            pltpu.SemaphoreType.DMA((5,)),
        ],
        name="pack",
    )(queries, out_grad, outputs, row_lse.reshape(4, BLOCK), collide.reshape(4, 8))
    pay = lax.ppermute(packed, "core", swap)
    ready = call(
        ready_kernel,
        (struct((8, 4, 128, 128), BF16), struct((8, 128, 128), F32), struct((8, 128), I32)),
        [VMEM] * 2, [pltpu.VMEM((128, 128), F32)], name="ready",
    )(packed, pay)
    part, dq_own, dq_other = call(
        main_kernel,
        (struct((4096, DH), BF16), struct((512, DH), F32), struct((512, DH), F32)),
        [VMEM] * 4,
        [
            pltpu.VMEM((17, 2, 128, 128), F32),
            pltpu.VMEM((9, 128, 128), F32),
            pltpu.VMEM((4096, DH), BF16),
            pltpu.SMEM((8, 128), I32),
            pltpu.SMEM((64 + 16 + 2 * PAIRS,), I32),
            pltpu.SemaphoreType.DMA,
            pltpu.SemaphoreType.DMA((4,)),
        ],
        name="attend",
        limit=16,
        outs_at=(HBM, VMEM, VMEM),
    )(gathered.reshape(4096, 128), *ready)
    got = exchange(part)
    query_grad = call(dq_kernel, struct((512, DH), BF16), [VMEM] * 2, name="dq")(
        dq_own, lax.ppermute(dq_other, "core", swap)
    )
    kv_grad = call(sum_kernel, struct((2, 16, 512), F32), [VMEM], name="total")(got.reshape(32, 128, 128))
    return query_grad, kv_grad.transpose(0, 2, 1)


def solution(mesh):
    fine = Mesh(
        mesh.devices.reshape(2, 4, KVH, 2, 2, 2), ("yh", "x", "group", "zl", "yl", "core")
    )
    ctx, head = ("yh", "x"), ("group", "zl", "yl", "core")
    placed = (
        P(ctx, head), P(ctx, head), P(ctx, head), P(None, ctx, head), P(head, ctx), P(head, ctx, None),
    )
    return jax.shard_map(
        shards, mesh=fine, in_specs=placed, out_specs=(P(ctx, head), P(None, ctx, head)),
        check_vma=False,
    )
```

```python
import jax
import jax.numpy as jnp
from jax import lax
from jax.experimental import pallas as pl
from jax.experimental.pallas import tpu as pltpu
from jax.sharding import Mesh, PartitionSpec as P

KVH = 8
DH = 128
BLOCK = 128
F32 = jnp.float32
BF16 = jnp.bfloat16
I32 = jnp.int32
SCALE = DH ** -0.5
PAIRS = 6
LOG2E = 1.4426950408889634
DEVICES = ("x", "yl", "zl", "yh", "core")
HBM = pl.BlockSpec(memory_space=pltpu.MemorySpace.HBM)
VMEM = pl.BlockSpec(memory_space=pltpu.VMEM)
ROW_Q, ROW_G, ROW_S, ROWS = 0, 512, 1024, 1056


def call(kernel, outs, in_specs, scratch=(), limit=4, outs_at=None):
    return pl.pallas_call(
        kernel,
        out_shape=outs,
        in_specs=in_specs,
        out_specs=outs_at or jax.tree.map(lambda _: VMEM, outs),
        scratch_shapes=list(scratch),
        compiler_params=pltpu.CompilerParams(vmem_limit_bytes=limit * 2**20),
    )


def pieces(value):
    high = value.astype(BF16).astype(F32)
    rest = value - high
    middle = rest.astype(BF16).astype(F32)
    return high, middle, rest - middle


def pack_kernel(q_ref, g_ref, o_ref, lse_ref, ids_ref, out_ref, o_v, lse_v, ids_v, small, sems):
    copies = [
        pltpu.make_async_copy(source, target, sems.at[n])
        for n, (source, target) in enumerate((
            (lse_ref, lse_v),
            (ids_ref, ids_v),
            (q_ref, out_ref.at[ROW_Q:ROW_G]),
            (g_ref, out_ref.at[ROW_G:ROW_S]),
            (o_ref, o_v),
        ))
    ]
    for copy in copies:
        copy.start()
    small[...] = jnp.zeros((32, 128), F32)
    for copy in copies:
        copy.wait()
    lane = lax.broadcasted_iota(I32, (128, 128), 1)
    columns = jnp.zeros((128, 128), F32)
    for b in range(4):
        rows = slice(b * 128, b * 128 + 128)
        g = out_ref[ROW_G + b * 128 : ROW_G + b * 128 + 128]
        delta = jnp.sum(g.astype(F32) * o_v[rows].astype(F32), axis=1, keepdims=True)
        columns = jnp.where(lane == b, delta, columns)
    for n, piece in enumerate(pieces(lse_v[...]) + pieces(columns.T[0:4])):
        small[n * 4 : n * 4 + 4] = piece
    small[24:28, 0:8] = ids_v[...].astype(F32)
    out_ref[ROW_S:ROWS] = small[...].astype(BF16)


def spread_kernel(kv_ref, out_ref, chunk, sems):
    for zl in range(2):
        for core in range(2):
            for which in range(2):
                column = (zl * 2 + core) * 128
                value = kv_ref[which, :, column : column + 128]
                for n in range(2):
                    for yh in range(2):
                        at = n * 256 + zl * 128 + yh * 64 + core * 32 + which * 16
                        chunk[at : at + 16] = value
    copies = [
        pltpu.make_async_copy(chunk, out_ref.at[n * 512 : n * 512 + 512], sems.at[n]) for n in range(4)
    ]
    for copy in copies:
        copy.start()
    for copy in copies:
        copy.wait()


SPAN = 448
NONE = 8
NO_PAIR = NONE + (16 << 14)


def ready_kernel(*refs):
    packed, (turned_ref, columns_ref, words_ref, table) = refs[:4], refs[4:]
    mine = lax.axis_index("zl") * 2 + lax.axis_index("core")
    table[...] = jnp.zeros((128, 128), F32)
    for n, ref in enumerate(packed):
        small = ref[ROW_S:ROWS].astype(F32)
        table[n * 4 : n * 4 + 4] = (small[0:4] + small[4:8] + small[8:12]) * LOG2E
        table[16 + n * 4 : 20 + n * 4] = small[12:16] + small[16:20] + small[20:24]
        table[32 + n * 4 : 36 + n * 4] = small[24:28]
        for b in range(4):
            for which, row in enumerate((ROW_Q, ROW_G)):
                turned_ref[n * 4 + b, which] = ref[row + b * 128 : row + b * 128 + 128].T
    block = table[32:48].astype(I32)
    row = lax.broadcasted_iota(I32, block.shape, 0)
    word = ((block >> 2) & 3) * 512 + (block >> 4) * 64 + (block >> 2) + (row << 14) + (1 << 20)
    words_ref[...] = jnp.where((block & 3) == mine, word, NONE)
    columns_ref[...] = table[...].T


def main_kernel(
    kv_ref, own_ref, near_ref, far_ref, last_ref, turned_ref, columns_ref, words_ref,
    part_ref, dq_near_ref, dq_far_ref,
    plain, level, acc, dq_acc, part, words_s, slots, sem, part_sems,
):
    copy = pltpu.make_async_copy(words_ref, words_s, sem)
    copy.start()
    for n, ref in enumerate((own_ref, near_ref, far_ref, last_ref)):
        for b in range(4):
            for which, row in enumerate((ROW_Q, ROW_G)):
                plain[n * 4 + b, which] = ref[row + b * 128 : row + b * 128 + 128]
    copy.wait()
    for b in range(16):
        for which in range(2):
            n = which * 16 + b
            level[b, which] = jnp.broadcast_to(columns_ref[:, n : n + 1], (128, 128))
    acc[...] = jnp.zeros(acc.shape, F32)
    dq_acc[...] = jnp.zeros(dq_acc.shape, F32)
    slot = jnp.int32(0)
    for b in range(16):
        for r in range(8):
            word = words_s[b, r]
            slots[slot] = word
            slot = slot + (word >> 20)
        slots[slot] = NONE
        slot = (slot + 1) & -2
    for p in range(2 * PAIRS):
        slots[slot + p] = NO_PAIR

    def tiles(words, which):
        columns = []
        for word in words:
            block = kv_ref.at[pl.ds(pl.multiple_of(word & 1984, 64), SPAN)]
            at = [yl * 256 + zl * 128 + core * 32 + which * 16 for zl in range(2) for yl in range(2) for core in range(2)]
            columns.append(jnp.concatenate([block[n : n + 16] for n in at], 0))
        return jnp.concatenate(columns, 1)

    def step(group, carry):
        begun = []
        for u in range(PAIRS):
            at = (group * PAIRS + u) * 2
            words = slots[at], slots[at + 1]
            b = (words[0] >> 14) & 15
            k = tiles(words, 0)
            scores = jnp.dot(plain[b, 0], k, preferred_element_type=F32)
            weight_grad = jnp.dot(plain[b, 1], tiles(words, 1), preferred_element_type=F32)
            lse, delta = level[b, 0], level[b, 1]
            weights, score_grads = [], []
            for n in range(2):
                cols = slice(n * 128, n * 128 + 128)
                weight = jnp.exp2(scores[:, cols] * (SCALE * LOG2E) - lse)
                score_grad = (weight * (weight_grad[:, cols] - delta) * SCALE).astype(BF16)
                if n:
                    score_grad = jnp.where((words[1] & 15) < NONE, score_grad, jnp.zeros_like(score_grad))
                weights.append(weight.astype(BF16))
                score_grads.append(score_grad)
            begun.append((words, b, k, jnp.concatenate(weights, 1), jnp.concatenate(score_grads, 1)))
        for words, b, k, weights, score_grad in begun:
            dq = lax.dot_general(score_grad, k, (((1,), (1,)), ((), ())), preferred_element_type=F32)
            dk = jnp.dot(turned_ref[b, 0], score_grad, preferred_element_type=F32)
            dv = jnp.dot(turned_ref[b, 1], weights, preferred_element_type=F32)
            dq_acc[(words[0] >> 14) & 31] += dq
            first, second = words[0] & 15, words[1] & 15
            old = [acc[n, which] for n in (first, second) for which in range(2)]
            new = [dk[:, :128], dv[:, :128], dk[:, 128:], dv[:, 128:]]
            new = [x + y for x, y in zip(old, new)]
            acc[first, 0], acc[first, 1], acc[second, 0], acc[second, 1] = new
        return carry

    lax.fori_loop(0, ((slot >> 1) + PAIRS - 1) // PAIRS, step, 0)
    copies = []
    for x in range(4):
        for yl in range(2):
            for zl in range(2):
                for yh in range(2):
                    for core in range(2):
                        for which in range(2):
                            at = x * 512 + yl * 256 + zl * 128 + yh * 64 + core * 32 + which * 16
                            feature = (zl * 2 + yl) * 32 + core * 16
                            tile = acc[yh * 4 + x, which, feature : feature + 16]
                            part[at : at + 16] = tile.astype(BF16)
        rows = slice(x * 512, x * 512 + 512)
        copies.append(pltpu.make_async_copy(part.at[rows], part_ref.at[rows], part_sems.at[x]))
        copies[-1].start()
    for b in range(8):
        dq_near_ref[b * 128 : b * 128 + 128] = dq_acc[b]
        dq_far_ref[b * 128 : b * 128 + 128] = dq_acc[b + 8].astype(BF16)
    for copy in copies:
        copy.wait()


def add_kernel(near_ref, got_ref, own_ref, other_ref):
    own_ref[...] = near_ref[0:512] + got_ref[0:512].astype(F32)
    other_ref[...] = near_ref[512:1024] + got_ref[512:1024].astype(F32)


def dq_kernel(own_ref, got_ref, out_ref):
    out_ref[...] = (own_ref[...] + got_ref[...]).astype(BF16)


def sum_kernel(got_ref, out_ref):
    for zl in range(2):
        for core in range(2):
            for which in range(2):
                value = jnp.zeros((16, 128), F32)
                for x in range(4):
                    for yl in range(2):
                        for yh in range(2):
                            at = x * 512 + yl * 256 + zl * 128 + yh * 64 + core * 32 + which * 16
                            value = value + got_ref[at : at + 16].astype(F32)
                column = (zl * 2 + core) * 128
                out_ref[which, :, column : column + 128] = value


def backward(queries, outputs, out_grad, keys_values, row_lse, collide):
    swap = [(0, 1), (1, 0)]
    struct = jax.ShapeDtypeStruct

    def exchange(value):
        return lax.all_to_all(value.reshape(64, 32, 128), DEVICES, 0, 0).reshape(2048, 128)

    packed = call(
        pack_kernel, struct((ROWS, DH), BF16), [HBM] * 5,
        [
            pltpu.VMEM((512, DH), BF16),
            pltpu.VMEM((4, 128), F32),
            pltpu.VMEM((4, 8), I32),
            pltpu.VMEM((32, 128), F32),
            pltpu.SemaphoreType.DMA((5,)),
        ],
        limit=60,
    )(queries, out_grad, outputs, row_lse.reshape(4, BLOCK), collide.reshape(4, 8))
    far = lax.ppermute(packed, "zl", swap)
    spread = call(
        spread_kernel, struct((2048, 128), BF16), [VMEM],
        [pltpu.VMEM((512, 128), BF16), pltpu.SemaphoreType.DMA((4,))],
        outs_at=HBM,
    )(keys_values.transpose(0, 2, 1))
    gathered = exchange(spread)
    queries_of = packed, lax.ppermute(packed, "core", swap), far, lax.ppermute(far, "core", swap)
    ready = call(
        ready_kernel,
        (struct((16, 2, 128, 128), BF16), struct((128, 128), F32), struct((16, 128), I32)),
        [VMEM] * 4, [pltpu.VMEM((128, 128), F32)],
    )(*queries_of)
    part, dq_near, dq_far = call(
        main_kernel,
        (struct((2048, DH), BF16), struct((1024, DH), F32), struct((1024, DH), BF16)),
        [VMEM] * 8,
        [
            pltpu.VMEM((16, 2, 128, 128), BF16),
            pltpu.VMEM((16, 2, 128, 128), F32),
            pltpu.VMEM((9, 2, 128, 128), F32),
            pltpu.VMEM((17, 128, 128), F32),
            pltpu.VMEM((2048, DH), BF16),
            pltpu.SMEM((16, 128), I32),
            pltpu.SMEM((128 + 32 + 2 * PAIRS,), I32),
            pltpu.SemaphoreType.DMA,
            pltpu.SemaphoreType.DMA((4,)),
        ],
        limit=16,
        outs_at=(HBM, VMEM, VMEM),
    )(gathered, *queries_of, *ready)
    got_dq = lax.ppermute(dq_far, "zl", swap)
    got = exchange(part)
    half = struct((512, DH), F32)
    dq_own, dq_other = call(add_kernel, (half, half), [VMEM] * 2)(dq_near, got_dq)
    query_grad = call(dq_kernel, struct((512, DH), BF16), [VMEM] * 2)(dq_own, lax.ppermute(dq_other, "core", swap))
    kv_grad = call(sum_kernel, struct((2, 16, 512), F32), [VMEM])(got)
    return query_grad, kv_grad.transpose(0, 2, 1)


def solution(mesh):
    fine = Mesh(
        mesh.devices.reshape(2, 4, KVH, 2, 2, 2), ("yh", "x", "group", "zl", "yl", "core")
    )
    ctx, head = ("yh", "x"), ("group", "zl", "yl", "core")
    placed = (
        P(ctx, head), P(ctx, head), P(ctx, head), P(None, ctx, head), P(head, ctx), P(head, ctx, None),
    )
    return jax.shard_map(
        backward, mesh=fine, in_specs=placed, out_specs=(P(ctx, head), P(None, ctx, head)),
        check_vma=False,
    )
```

```python
import jax
import jax.numpy as jnp
from jax import lax
from jax.experimental import pallas as pl
from jax.experimental.pallas import tpu as pltpu
from jax.sharding import Mesh, PartitionSpec as P

KVH = 8
DH = 128
BLOCK = 128
F32 = jnp.float32
BF16 = jnp.bfloat16
I32 = jnp.int32
SCALE = DH ** -0.5
PAIRS = 6
LOG2E = 1.4426950408889634
DEVICES = ("x", "yl", "zl", "yh", "core")
HBM = pl.BlockSpec(memory_space=pltpu.MemorySpace.HBM)
VMEM = pl.BlockSpec(memory_space=pltpu.VMEM)
ROW_Q, ROW_G, ROW_S, ROWS = 0, 512, 1024, 1056


def call(kernel, outs, in_specs, scratch=(), limit=4, outs_at=None):
    return pl.pallas_call(
        kernel,
        out_shape=outs,
        in_specs=in_specs,
        out_specs=outs_at or jax.tree.map(lambda _: VMEM, outs),
        scratch_shapes=list(scratch),
        compiler_params=pltpu.CompilerParams(vmem_limit_bytes=limit * 2**20),
    )


def pieces(value):
    high = value.astype(BF16).astype(F32)
    rest = value - high
    middle = rest.astype(BF16).astype(F32)
    return high, middle, rest - middle


def pack_kernel(
    q_ref, g_ref, o_ref, lse_ref, ids_ref, kv_ref, out_ref, spread_ref,
    o_v, lse_v, ids_v, kv_v, small, chunk, sems,
):
    copies = [
        pltpu.make_async_copy(source, target, sems.at[n])
        for n, (source, target) in enumerate((
            (kv_ref, kv_v),
            (lse_ref, lse_v),
            (ids_ref, ids_v),
            (g_ref, out_ref.at[ROW_G:ROW_S]),
            (o_ref, o_v),
            (q_ref, out_ref.at[ROW_Q:ROW_G]),
        ))
    ]
    for copy in copies:
        copy.start()
    small[...] = jnp.zeros((32, 128), F32)
    copies[0].wait()
    for zl in range(2):
        for core in range(2):
            for which in range(2):
                column = (zl * 2 + core) * 128
                value = kv_v[which, :, column : column + 128]
                for n in range(2):
                    for yh in range(2):
                        at = n * 256 + zl * 128 + yh * 64 + core * 32 + which * 16
                        chunk[at : at + 16] = value
    spreads = [
        pltpu.make_async_copy(chunk, spread_ref.at[n * 512 : n * 512 + 512], sems.at[6 + n]) for n in range(4)
    ]
    for copy in spreads:
        copy.start()
    for copy in copies[1:]:
        copy.wait()
    lane = lax.broadcasted_iota(I32, (128, 128), 1)
    columns = jnp.zeros((128, 128), F32)
    for b in range(4):
        rows = slice(b * 128, b * 128 + 128)
        g = out_ref[ROW_G + b * 128 : ROW_G + b * 128 + 128]
        delta = jnp.sum(g.astype(F32) * o_v[rows].astype(F32), axis=1, keepdims=True)
        columns = jnp.where(lane == b, delta, columns)
    for n, piece in enumerate(pieces(lse_v[...]) + pieces(columns.T[0:4])):
        small[n * 4 : n * 4 + 4] = piece
    small[24:28, 0:8] = ids_v[...].astype(F32)
    out_ref[ROW_S:ROWS] = small[...].astype(BF16)
    for copy in spreads:
        copy.wait()


SPAN = 448
NONE = 8
NO_PAIR = NONE + (16 << 14)


def ready_kernel(*refs):
    packed, (turned_ref, columns_ref, words_ref, table) = refs[:4], refs[4:]
    mine = lax.axis_index("zl") * 2 + lax.axis_index("core")
    table[...] = jnp.zeros((128, 128), F32)
    for n, ref in enumerate(packed):
        small = ref[ROW_S:ROWS].astype(F32)
        table[n * 4 : n * 4 + 4] = (small[0:4] + small[4:8] + small[8:12]) * LOG2E
        table[16 + n * 4 : 20 + n * 4] = small[12:16] + small[16:20] + small[20:24]
        table[32 + n * 4 : 36 + n * 4] = small[24:28]
        for b in range(4):
            for which, row in enumerate((ROW_Q, ROW_G)):
                turned_ref[n * 4 + b, which] = ref[row + b * 128 : row + b * 128 + 128].T
    block = table[32:48].astype(I32)
    row = lax.broadcasted_iota(I32, block.shape, 0)
    word = ((block >> 2) & 3) * 512 + (block >> 4) * 64 + (block >> 2) + (row << 14) + (1 << 20)
    words_ref[...] = jnp.where((block & 3) == mine, word, NONE)
    columns_ref[...] = table[...].T


def main_kernel(
    kv_ref, own_ref, near_ref, far_ref, last_ref, turned_ref, columns_ref, words_ref,
    acc, dq_near_ref, dq_far_ref,
    plain, dq_acc, words_s, slots, sem,
):
    copy = pltpu.make_async_copy(words_ref, words_s, sem)
    copy.start()
    for n, ref in enumerate((own_ref, near_ref, far_ref, last_ref)):
        for b in range(4):
            for which, row in enumerate((ROW_Q, ROW_G)):
                plain[n * 4 + b, which] = ref[row + b * 128 : row + b * 128 + 128]
    copy.wait()
    acc[...] = jnp.zeros(acc.shape, F32)
    dq_acc[...] = jnp.zeros(dq_acc.shape, F32)
    slot = jnp.int32(0)
    for b in range(16):
        for r in range(8):
            word = words_s[b, r]
            slots[slot] = word
            slot = slot + (word >> 20)
        slots[slot] = NONE
        slot = (slot + 1) & -2
    for p in range(2 * PAIRS):
        slots[slot + p] = NO_PAIR

    def tiles(words, which):
        columns = []
        for word in words:
            block = kv_ref.at[pl.ds(pl.multiple_of(word & 1984, 64), SPAN)]
            at = [yl * 256 + zl * 128 + core * 32 + which * 16 for zl in range(2) for yl in range(2) for core in range(2)]
            columns.append(jnp.concatenate([block[n : n + 16] for n in at], 0))
        return jnp.concatenate(columns, 1)

    def step(group, carry):
        begun = []
        for u in range(PAIRS):
            at = (group * PAIRS + u) * 2
            words = slots[at], slots[at + 1]
            b = (words[0] >> 14) & 15
            k = tiles(words, 0)
            scores = jnp.dot(plain[b, 0], k, preferred_element_type=F32)
            weight_grad = jnp.dot(plain[b, 1], tiles(words, 1), preferred_element_type=F32)
            lse, delta = (
                jnp.take_along_axis(columns_ref[...], jnp.full((128, 128), n, I32), axis=1) for n in (b, 16 + b)
            )
            weights, score_grads = [], []
            for n in range(2):
                cols = slice(n * 128, n * 128 + 128)
                weight = jnp.exp2(scores[:, cols] * (SCALE * LOG2E) - lse)
                score_grad = (weight * (weight_grad[:, cols] - delta) * SCALE).astype(BF16)
                if n:
                    score_grad = jnp.where((words[1] & 15) < NONE, score_grad, jnp.zeros_like(score_grad))
                weights.append(weight.astype(BF16))
                score_grads.append(score_grad)
            begun.append((words, b, k, jnp.concatenate(weights, 1), jnp.concatenate(score_grads, 1)))
        for words, b, k, weights, score_grad in begun:
            dq = lax.dot_general(score_grad, k, (((1,), (1,)), ((), ())), preferred_element_type=F32)
            dk = jnp.dot(turned_ref[b, 0], score_grad, preferred_element_type=F32)
            dv = jnp.dot(turned_ref[b, 1], weights, preferred_element_type=F32)
            dq_acc[(words[0] >> 14) & 31] += dq
            first, second = words[0] & 15, words[1] & 15
            old = [acc[n, which] for n in (first, second) for which in range(2)]
            new = [dk[:, :128], dv[:, :128], dk[:, 128:], dv[:, 128:]]
            new = [x + y for x, y in zip(old, new)]
            acc[first, 0], acc[first, 1], acc[second, 0], acc[second, 1] = new
        return carry

    lax.fori_loop(0, ((slot >> 1) + PAIRS - 1) // PAIRS, step, 0)
    for b in range(8):
        dq_near_ref[b * 128 : b * 128 + 128] = dq_acc[b]
        dq_far_ref[b * 128 : b * 128 + 128] = dq_acc[b + 8].astype(BF16)


def partial_kernel(acc, part_ref, part, sems):
    copies = []
    for x in range(4):
        for yl in range(2):
            for zl in range(2):
                for yh in range(2):
                    for core in range(2):
                        for which in range(2):
                            at = x * 512 + yl * 256 + zl * 128 + yh * 64 + core * 32 + which * 16
                            feature = (zl * 2 + yl) * 32 + core * 16
                            tile = acc[yh * 4 + x, which, feature : feature + 16]
                            part[at : at + 16] = tile.astype(BF16)
        rows = slice(x * 512, x * 512 + 512)
        copies.append(pltpu.make_async_copy(part.at[rows], part_ref.at[rows], sems.at[x]))
        copies[-1].start()
    for copy in copies:
        copy.wait()


def add_kernel(near_ref, got_ref, own_ref, other_ref):
    own_ref[...] = near_ref[0:512] + got_ref[0:512].astype(F32)
    other_ref[...] = near_ref[512:1024] + got_ref[512:1024].astype(F32)


def dq_kernel(own_ref, got_ref, out_ref):
    out_ref[...] = (own_ref[...] + got_ref[...]).astype(BF16)


def sum_kernel(got_ref, out_ref):
    for zl in range(2):
        for core in range(2):
            for which in range(2):
                value = jnp.zeros((16, 128), F32)
                for x in range(4):
                    for yl in range(2):
                        for yh in range(2):
                            at = x * 512 + yl * 256 + zl * 128 + yh * 64 + core * 32 + which * 16
                            value = value + got_ref[at : at + 16].astype(F32)
                column = (zl * 2 + core) * 128
                out_ref[which, :, column : column + 128] = value


def backward(queries, outputs, out_grad, keys_values, row_lse, collide):
    swap = [(0, 1), (1, 0)]
    struct = jax.ShapeDtypeStruct

    def exchange(value):
        return lax.all_to_all(value.reshape(64, 32, 128), DEVICES, 0, 0).reshape(2048, 128)

    packed, spread = call(
        pack_kernel, (struct((ROWS, DH), BF16), struct((2048, DH), BF16)), [HBM] * 6,
        [
            pltpu.VMEM((512, DH), BF16),
            pltpu.VMEM((4, 128), F32),
            pltpu.VMEM((4, 8), I32),
            pltpu.VMEM((2, 16, 512), BF16),
            pltpu.VMEM((32, 128), F32),
            pltpu.VMEM((512, DH), BF16),
            pltpu.SemaphoreType.DMA((10,)),
        ],
        limit=60,
        outs_at=(VMEM, HBM),
    )(
        queries, out_grad, outputs, row_lse.reshape(4, BLOCK), collide.reshape(4, 8),
        keys_values.transpose(0, 2, 1),
    )
    far = lax.ppermute(packed, "zl", swap)
    gathered = exchange(spread)
    queries_of = packed, lax.ppermute(packed, "core", swap), far, lax.ppermute(far, "core", swap)
    ready = call(
        ready_kernel,
        (struct((16, 2, 128, 128), BF16), struct((128, 128), F32), struct((16, 128), I32)),
        [VMEM] * 4, [pltpu.VMEM((128, 128), F32)],
    )(*queries_of)
    sums, dq_near, dq_far = call(
        main_kernel,
        (struct((9, 2, 128, 128), F32), struct((1024, DH), F32), struct((1024, DH), BF16)),
        [VMEM] * 8,
        [
            pltpu.VMEM((16, 2, 128, 128), BF16),
            pltpu.VMEM((17, 128, 128), F32),
            pltpu.SMEM((16, 128), I32),
            pltpu.SMEM((128 + 32 + 2 * PAIRS,), I32),
            pltpu.SemaphoreType.DMA,
        ],
        limit=16,
    )(gathered, *queries_of, *ready)
    got_dq = lax.ppermute(dq_far, "zl", swap)
    part = call(
        partial_kernel, struct((2048, DH), BF16), [VMEM],
        [pltpu.VMEM((2048, DH), BF16), pltpu.SemaphoreType.DMA((4,))], outs_at=HBM,
    )(sums)
    got = exchange(part)
    half = struct((512, DH), F32)
    dq_own, dq_other = call(add_kernel, (half, half), [VMEM] * 2)(dq_near, got_dq)
    query_grad = call(dq_kernel, struct((512, DH), BF16), [VMEM] * 2)(dq_own, lax.ppermute(dq_other, "core", swap))
    kv_grad = call(sum_kernel, struct((2, 16, 512), F32), [VMEM])(got)
    return query_grad, kv_grad.transpose(0, 2, 1)


def solution(mesh):
    fine = Mesh(
        mesh.devices.reshape(2, 4, KVH, 2, 2, 2), ("yh", "x", "group", "zl", "yl", "core")
    )
    ctx, head = ("yh", "x"), ("group", "zl", "yl", "core")
    placed = (
        P(ctx, head), P(ctx, head), P(ctx, head), P(None, ctx, head), P(head, ctx), P(head, ctx, None),
    )
    return jax.shard_map(
        backward, mesh=fine, in_specs=placed, out_specs=(P(ctx, head), P(None, ctx, head)),
        check_vma=False,
    )
```

```python
import jax
import jax.numpy as jnp
from jax import lax
from jax.experimental import pallas as pl
from jax.experimental.pallas import tpu as pltpu
from jax.sharding import Mesh, PartitionSpec as P

KVH = 8
DH = 128
BLOCK = 128
F32 = jnp.float32
BF16 = jnp.bfloat16
I32 = jnp.int32
SCALE = DH ** -0.5
PAIRS = 9
LOG2E = 1.4426950408889634
DEVICES = ("x", "yl", "zl", "yh", "core")
HBM = pl.BlockSpec(memory_space=pltpu.MemorySpace.HBM)
VMEM = pl.BlockSpec(memory_space=pltpu.VMEM)
ROW_Q, ROW_G, ROW_S, ROWS = 0, 512, 1024, 1056


def call(kernel, outs, in_specs, scratch=(), limit=4, outs_at=None):
    return pl.pallas_call(
        kernel,
        out_shape=outs,
        in_specs=in_specs,
        out_specs=outs_at or jax.tree.map(lambda _: VMEM, outs),
        scratch_shapes=list(scratch),
        compiler_params=pltpu.CompilerParams(vmem_limit_bytes=limit * 2**20),
    )


def pieces(value):
    high = value.astype(BF16).astype(F32)
    rest = value - high
    middle = rest.astype(BF16).astype(F32)
    return high, middle, rest - middle


def pack_kernel(
    q_ref, g_ref, o_ref, lse_ref, ids_ref, kv_ref, out_ref, spread_ref,
    out_v, o_v, lse_v, ids_v, kv_v, small, chunk, sems,
):
    copies = [
        pltpu.make_async_copy(source, target, sems.at[n])
        for n, (source, target) in enumerate((
            (kv_ref, kv_v),
            (lse_ref, lse_v),
            (ids_ref, ids_v),
            (g_ref, out_v.at[ROW_G:ROW_S]),
            (o_ref, o_v),
            (q_ref, out_v.at[ROW_Q:ROW_G]),
        ))
    ]
    for copy in copies:
        copy.start()
    small[...] = jnp.zeros((32, 128), F32)
    copies[0].wait()
    for zl in range(2):
        for core in range(2):
            for which in range(2):
                column = (zl * 2 + core) * 128
                value = kv_v[which, :, column : column + 128]
                for n in range(2):
                    for yh in range(2):
                        at = n * 256 + zl * 128 + yh * 64 + core * 32 + which * 16
                        chunk[at : at + 16] = value
    spreads = [
        pltpu.make_async_copy(chunk, spread_ref.at[n * 512 : n * 512 + 512], sems.at[6 + n]) for n in range(4)
    ]
    for copy in spreads:
        copy.start()
    for copy in copies[1:]:
        copy.wait()
    spreads += [
        pltpu.make_async_copy(out_v.at[rows], out_ref.at[rows], sems.at[10 + n])
        for n, rows in enumerate((slice(ROW_Q, ROW_S), slice(ROW_S, ROWS)))
    ]
    spreads[4].start()
    lane = lax.broadcasted_iota(I32, (128, 128), 1)
    columns = jnp.zeros((128, 128), F32)
    for b in range(4):
        rows = slice(b * 128, b * 128 + 128)
        g = out_v[ROW_G + b * 128 : ROW_G + b * 128 + 128]
        delta = jnp.sum(g.astype(F32) * o_v[rows].astype(F32), axis=1, keepdims=True)
        columns = jnp.where(lane == b, delta, columns)
    for n, piece in enumerate(pieces(lse_v[...]) + pieces(columns.T[0:4])):
        small[n * 4 : n * 4 + 4] = piece
    small[24:28, 0:8] = ids_v[...].astype(F32)
    out_v[ROW_S:ROWS] = small[...].astype(BF16)
    spreads[5].start()
    for copy in spreads:
        copy.wait()


SPAN = 448
NONE = 8
NO_PAIR = NONE + (16 << 14)


def ready_kernel(*refs):
    packed, (turned_ref, columns_ref, words_ref, table) = refs[:4], refs[4:]
    mine = lax.axis_index("zl") * 2 + lax.axis_index("core")
    table[...] = jnp.zeros((128, 128), F32)
    for n, ref in enumerate(packed):
        small = ref[ROW_S:ROWS].astype(F32)
        table[n * 4 : n * 4 + 4] = (small[0:4] + small[4:8] + small[8:12]) * LOG2E
        table[16 + n * 4 : 20 + n * 4] = small[12:16] + small[16:20] + small[20:24]
        table[32 + n * 4 : 36 + n * 4] = small[24:28]
        for b in range(4):
            for which, row in enumerate((ROW_Q, ROW_G)):
                turned_ref[n * 4 + b, which] = ref[row + b * 128 : row + b * 128 + 128].T
    block = table[32:48].astype(I32)
    row = lax.broadcasted_iota(I32, block.shape, 0)
    word = ((block >> 2) & 3) * 512 + (block >> 4) * 64 + (block >> 2) + (row << 14) + (1 << 20)
    words_ref[...] = jnp.where((block & 3) == mine, word, NONE)
    columns_ref[...] = table[...].T


def main_kernel(
    kv_ref, own_ref, near_ref, far_ref, last_ref, turned_ref, columns_ref, words_ref,
    acc, dq_near_ref, dq_far_ref,
    plain, dq_acc, words_s, slots, sem,
):
    copy = pltpu.make_async_copy(words_ref, words_s, sem)
    copy.start()
    for n, ref in enumerate((own_ref, near_ref, far_ref, last_ref)):
        for b in range(4):
            for which, row in enumerate((ROW_Q, ROW_G)):
                plain[n * 4 + b, which] = ref[row + b * 128 : row + b * 128 + 128]
    copy.wait()
    acc[...] = jnp.zeros(acc.shape, F32)
    dq_acc[...] = jnp.zeros(dq_acc.shape, F32)
    slot = jnp.int32(0)
    for b in range(16):
        for r in range(8):
            word = words_s[b, r]
            slots[slot] = word
            slot = slot + (word >> 20)
        slots[slot] = NONE
        slot = (slot + 1) & -2
    for p in range(2 * PAIRS):
        slots[slot + p] = NO_PAIR

    def tiles(words, which):
        columns = []
        for word in words:
            block = kv_ref.at[pl.ds(pl.multiple_of(word & 1984, 64), SPAN)]
            at = [yl * 256 + zl * 128 + core * 32 + which * 16 for zl in range(2) for yl in range(2) for core in range(2)]
            columns.append(jnp.concatenate([block[n : n + 16] for n in at], 0))
        return jnp.concatenate(columns, 1)

    def step(group, carry):
        begun = []
        for u in range(PAIRS):
            at = (group * PAIRS + u) * 2
            words = slots[at], slots[at + 1]
            b = (words[0] >> 14) & 15
            k = tiles(words, 0)
            scores = jnp.dot(plain[b, 0], k, preferred_element_type=F32)
            weight_grad = jnp.dot(plain[b, 1], tiles(words, 1), preferred_element_type=F32)
            lse, delta = (
                jnp.take_along_axis(columns_ref[...], jnp.full((128, 128), n, I32), axis=1) for n in (b, 16 + b)
            )
            weights, score_grads = [], []
            for n in range(2):
                cols = slice(n * 128, n * 128 + 128)
                weight = jnp.exp2(scores[:, cols] * (SCALE * LOG2E) - lse)
                score_grad = (weight * (weight_grad[:, cols] - delta) * SCALE).astype(BF16)
                if n:
                    score_grad = jnp.where((words[1] & 15) < NONE, score_grad, jnp.zeros_like(score_grad))
                weights.append(weight.astype(BF16))
                score_grads.append(score_grad)
            begun.append((words, b, k, jnp.concatenate(weights, 1), jnp.concatenate(score_grads, 1)))
        for words, b, k, weights, score_grad in begun:
            dq = lax.dot_general(score_grad, k, (((1,), (1,)), ((), ())), preferred_element_type=F32)
            dk = jnp.dot(turned_ref[b, 0], score_grad, preferred_element_type=F32)
            dv = jnp.dot(turned_ref[b, 1], weights, preferred_element_type=F32)
            dq_acc[(words[0] >> 14) & 31] += dq
            first, second = words[0] & 15, words[1] & 15
            old = [acc[n, which] for n in (first, second) for which in range(2)]
            new = [dk[:, :128], dv[:, :128], dk[:, 128:], dv[:, 128:]]
            new = [x + y for x, y in zip(old, new)]
            acc[first, 0], acc[first, 1], acc[second, 0], acc[second, 1] = new
        return carry

    lax.fori_loop(0, ((slot >> 1) + PAIRS - 1) // PAIRS, step, 0)
    for b in range(8):
        dq_near_ref[b * 128 : b * 128 + 128] = dq_acc[b]
        dq_far_ref[b * 128 : b * 128 + 128] = dq_acc[b + 8].astype(BF16)


def partial_kernel(acc, part_ref, part, sems):
    copies = []
    for x in range(4):
        for yl in range(2):
            for zl in range(2):
                for yh in range(2):
                    for core in range(2):
                        for which in range(2):
                            at = x * 512 + yl * 256 + zl * 128 + yh * 64 + core * 32 + which * 16
                            feature = (zl * 2 + yl) * 32 + core * 16
                            tile = acc[yh * 4 + x, which, feature : feature + 16]
                            part[at : at + 16] = tile.astype(BF16)
        rows = slice(x * 512, x * 512 + 512)
        copies.append(pltpu.make_async_copy(part.at[rows], part_ref.at[rows], sems.at[x]))
        copies[-1].start()
    for copy in copies:
        copy.wait()


def add_kernel(near_ref, got_ref, own_ref, other_ref):
    own_ref[...] = near_ref[0:512] + got_ref[0:512].astype(F32)
    other_ref[...] = near_ref[512:1024] + got_ref[512:1024].astype(F32)


def dq_kernel(own_ref, got_ref, out_ref):
    out_ref[...] = (own_ref[...] + got_ref[...]).astype(BF16)


def sum_kernel(got_ref, out_ref):
    for zl in range(2):
        for core in range(2):
            for which in range(2):
                value = jnp.zeros((16, 128), F32)
                for x in range(4):
                    for yl in range(2):
                        for yh in range(2):
                            at = x * 512 + yl * 256 + zl * 128 + yh * 64 + core * 32 + which * 16
                            value = value + got_ref[at : at + 16].astype(F32)
                column = (zl * 2 + core) * 128
                out_ref[which, :, column : column + 128] = value


def backward(queries, outputs, out_grad, keys_values, row_lse, collide):
    swap = [(0, 1), (1, 0)]
    struct = jax.ShapeDtypeStruct

    def exchange(value):
        return lax.all_to_all(value.reshape(64, 32, 128), DEVICES, 0, 0).reshape(2048, 128)

    packed, spread = call(
        pack_kernel, (struct((ROWS, DH), BF16), struct((2048, DH), BF16)), [HBM] * 6,
        [
            pltpu.VMEM((ROWS, DH), BF16),
            pltpu.VMEM((512, DH), BF16),
            pltpu.VMEM((4, 128), F32),
            pltpu.VMEM((4, 8), I32),
            pltpu.VMEM((2, 16, 512), BF16),
            pltpu.VMEM((32, 128), F32),
            pltpu.VMEM((512, DH), BF16),
            pltpu.SemaphoreType.DMA((12,)),
        ],
        limit=60,
        outs_at=(HBM, HBM),
    )(
        queries, out_grad, outputs, row_lse.reshape(4, BLOCK), collide.reshape(4, 8),
        keys_values.transpose(0, 2, 1),
    )
    far = lax.ppermute(packed, "zl", swap)
    gathered = exchange(spread)
    queries_of = packed, lax.ppermute(packed, "core", swap), far, lax.ppermute(far, "core", swap)
    ready = call(
        ready_kernel,
        (struct((16, 2, 128, 128), BF16), struct((128, 128), F32), struct((16, 128), I32)),
        [VMEM] * 4, [pltpu.VMEM((128, 128), F32)],
    )(*queries_of)
    sums, dq_near, dq_far = call(
        main_kernel,
        (struct((9, 2, 128, 128), F32), struct((1024, DH), F32), struct((1024, DH), BF16)),
        [VMEM] * 8,
        [
            pltpu.VMEM((16, 2, 128, 128), BF16),
            pltpu.VMEM((17, 128, 128), F32),
            pltpu.SMEM((16, 128), I32),
            pltpu.SMEM((128 + 32 + 2 * PAIRS,), I32),
            pltpu.SemaphoreType.DMA,
        ],
        limit=16,
    )(gathered, *queries_of, *ready)
    got_dq = lax.ppermute(dq_far, "zl", swap)
    part = call(
        partial_kernel, struct((2048, DH), BF16), [VMEM],
        [pltpu.VMEM((2048, DH), BF16), pltpu.SemaphoreType.DMA((4,))], outs_at=HBM,
    )(sums)
    got = exchange(part)
    half = struct((512, DH), F32)
    dq_own, dq_other = call(add_kernel, (half, half), [VMEM] * 2)(dq_near, got_dq)
    query_grad = call(dq_kernel, struct((512, DH), BF16), [VMEM] * 2)(dq_own, lax.ppermute(dq_other, "core", swap))
    kv_grad = call(sum_kernel, struct((2, 16, 512), F32), [VMEM])(got)
    return query_grad, kv_grad.transpose(0, 2, 1)


def solution(mesh):
    fine = Mesh(
        mesh.devices.reshape(2, 4, KVH, 2, 2, 2), ("yh", "x", "group", "zl", "yl", "core")
    )
    ctx, head = ("yh", "x"), ("group", "zl", "yl", "core")
    placed = (
        P(ctx, head), P(ctx, head), P(ctx, head), P(None, ctx, head), P(head, ctx), P(head, ctx, None),
    )
    return jax.shard_map(
        backward, mesh=fine, in_specs=placed, out_specs=(P(ctx, head), P(None, ctx, head)),
        check_vma=False,
    )
```
